32 devices in a mesh: groups: 2 (over x), rows: 16 (over z, y, core).
Axes of the slice: x: 2, y: 2, z: 4, core: 2. Of those that a mesh axis runs over, the one named last changes fastest.
Arguments:
- row_leaves: int32 [32, 65536], P(None, ('groups', 'rows')), parts along dimension 1, may hold values from 0 to 127
- covariates: bfloat16 [64, 65536], P(None, ('groups', 'rows')), parts along dimension 1, may hold values from -6 to 6
- query_leaves: int32 [32, 128], P(None, 'groups'), parts along dimension 1, may hold values from 0 to 127
- leaf_sizes: int32 [64, 128], P('groups'), parts along dimension 0, may hold values from 128 to 511
Outputs:
- moments: float32 [128, 4096], P(('groups', 'rows')), parts along dimension 0
The draws below stay inside these ranges and needn't reach their ends.
There are 2 independent parts, one for each index of `groups`. The reference program is written for one: setup_inputs(seed, part) draws one part's arguments, and reference() takes and returns one part's arrays. A program takes and returns all parts, laid end to end along the dimension named above; each array names one. Nothing has to cross between parts.
All inputs are finite; a program needn't handle non-finite values.
Results may differ from the reference program's by a relative error of at most 0.0006.
Values may be sent and summed in bfloat16 or wider, within the bound.
A program may use at most 64 MiB of HBM per device.

```python
import math
import jax
import jax.numpy as jnp
import numpy as np
from jax import lax

P_SIZE = 64
LEAVES = 128
TREES = 32
ROWS = 32768
Q = 64


def touch_ends(drawn, stream_key, least, high):
    longest = drawn.shape.index(max(drawn.shape))
    spots = []
    for shift in (0, 1):
        where = [jax.random.randint(jax.random.fold_in(stream_key, axis), (), 0, length) for axis, length in enumerate(drawn.shape)]
        where[longest] = (where[longest] + shift) % drawn.shape[longest]
        spots.append(tuple(where))
    return drawn.at[spots[0]].set(least).at[spots[1]].set(high)


def level_of(rng, dims, shards, low, largest):
    loudness = 1.0
    for dim, blocks in shards:
        heights = jax.random.uniform(jax.random.fold_in(jax.random.fold_in(rng, 6), dim), (blocks,), jnp.float32, low / len(shards), largest / len(shards))
        loudness = loudness * jnp.repeat(jnp.exp(heights), dims[dim] // blocks).reshape((-1,) + (1,) * (len(dims) - 1 - dim))
    return loudness


def cumulative_ranks(amount, slope):
    portions = [(1 << 20) // math.isqrt(grade ** slope) + 1 for grade in range(1, amount + 1)]
    width = 1 + sum(portions) // (1 << 30)
    return np.cumsum(np.array([max(1, weight // width) for weight in portions]))


def skewed_ids(own_key, shape, number_of, lean):
    listing = cumulative_ranks(number_of, lean)
    pick = jax.random.randint(jax.random.fold_in(own_key, 1), shape, 0, int(listing[number_of - 1]))
    standing = jnp.searchsorted(jnp.asarray(listing, jnp.int32), pick, side="right")
    return jax.random.permutation(jax.random.fold_in(own_key, 2), number_of)[standing].astype(jnp.int32)


def normal_values(own_key, shape, scale, reach, shards=(), held_as=jnp.bfloat16):
    entries = scale * jax.random.normal(own_key, shape, jnp.float32)
    if shards:
        entries = entries * level_of(own_key, shape, shards, -0.22, 0.18)
    return jnp.clip(entries, -reach, reach).astype(held_as)


def setup_inputs(seed: int = 0, part: int = 0) -> dict:
    splits = jax.random.split(jax.random.key(seed), 5)
    part_splits = jax.random.split(jax.random.fold_in(splits[4], part), 5)
    return {
        "row_leaves": touch_ends(jax.random.randint(part_splits[0], (TREES, ROWS), 0, LEAVES), jax.random.fold_in(part_splits[0], 1), 0, LEAVES - 1).astype(jnp.int32),
        "covariates": normal_values(part_splits[1], (P_SIZE, ROWS), 1.0, 6.0, ((1, 16),)),
        "query_leaves": touch_ends(skewed_ids(part_splits[2], (TREES, Q), LEAVES, 2), jax.random.fold_in(part_splits[2], 3), 0, LEAVES - 1).astype(jnp.int32),
        "leaf_sizes": touch_ends(jax.random.randint(part_splits[3], (TREES, LEAVES), ROWS // LEAVES // 2, 2 * ROWS // LEAVES), jax.random.fold_in(part_splits[3], 1), ROWS // LEAVES // 2, (2 * ROWS // LEAVES) - 1).astype(jnp.int32),
    }


def reference(row_leaves, covariates, query_leaves, leaf_sizes):
    inverse = 1.0 / (TREES * leaf_sizes.astype(jnp.float32))
    chosen = jnp.take_along_axis(inverse, query_leaves, axis=1).astype(jnp.bfloat16)
    chosen = lax.optimization_barrier(chosen).astype(jnp.float32)
    row_block = math.gcd(ROWS, 2048)
    count_blocks = ROWS // row_block
    leaf_blocks = jnp.transpose(row_leaves.reshape(TREES, count_blocks, row_block), (1, 0, 2))
    covar_blocks = jnp.transpose(covariates.reshape(P_SIZE, count_blocks, row_block), (1, 0, 2))

    def step(summed, inputs):
        leaf_block, covar_block = inputs
        match = query_leaves[:, :, None] == leaf_block[:, None, :]
        weights = jnp.sum(jnp.where(match, chosen[:, :, None], jnp.float32(0.0)), axis=0).astype(jnp.bfloat16)
        widened = covar_block.astype(jnp.float32)
        product = (widened[:, None, :] * widened[None, :, :]).reshape(P_SIZE * P_SIZE, row_block).astype(jnp.bfloat16)
        summed = summed + lax.dot_general(weights, product, (((1,), (1,)), ((), ())), preferred_element_type=jnp.float32)
        return summed, None

    summed, _ = lax.scan(step, jnp.zeros((Q, P_SIZE * P_SIZE), jnp.float32), (leaf_blocks, covar_blocks))
    return summed
```

```python
import functools

import jax
import jax.numpy as jnp
from jax import lax
from jax.experimental import pallas as pl
from jax.experimental.pallas import tpu as pltpu
from jax.sharding import PartitionSpec as P

CHUNKS = 4
GROUP = 4
LANES = 128


def kernel(n, rl_ref, x_ref, ql_ref, ls_ref, o_ref, xf, qb, wb, w_s, prod, part, s2, s3, r1, r2, r3,
           ss1, rs1, ss2, rs2, ss3, rs3):
    trees, rows = rl_ref.shape
    width = x_ref.shape[0]
    queries = ql_ref.shape[1]
    t = queries // n
    nz = n // 4
    sub = nz * t
    cols = width * width // CHUNKS
    me = lax.axis_index("rows")
    core = lax.rem(me, 2)
    y = lax.rem(me // 2, 2)
    z = me // 4

    sibling = me + 1 - 2 * core
    ypeer = me + 2 - 4 * y
    zpeers = [lax.rem(me + 4 * d, n) for d in range(1, nz)]
    barrier = pltpu.get_barrier_semaphore()
    for peer in [sibling, ypeer] + zpeers:
        pl.semaphore_signal(barrier, inc=1, device_id={"rows": peer}, device_id_type=pl.DeviceIdType.MESH)

    xf[...] = x_ref[...].astype(jnp.float32)

    inverse = 1.0 / (trees * ls_ref[...].astype(jnp.float32))
    ql = ql_ref[...]
    leaf_cols, weight_cols = [], []
    for first in range(0, queries, LANES):
        piece = ql[:, first:first + LANES]
        if piece.shape[1] < LANES:
            piece = jnp.concatenate([piece] * (LANES // piece.shape[1]), axis=1)
        chosen = jnp.take_along_axis(inverse, piece, axis=1).astype(jnp.bfloat16).astype(jnp.float32)
        leaf_cols.append(piece.T)
        weight_cols.append(chosen.T)

    def ordered(cols_list):
        out = []
        for c in range(2):
            for b in range(2):
                for k in range(nz):
                    first = (k * 4 + b * 2 + c) * t
                    out.append(cols_list[first // LANES][first % LANES:first % LANES + t])
        return jnp.concatenate(out, axis=0)

    leaf_t = ordered(leaf_cols)
    weight_t = ordered(weight_cols)
    for b in range(trees):
        qb[b] = jnp.broadcast_to(leaf_t[:, b:b + 1], (queries, LANES))
        wb[b] = jnp.broadcast_to(weight_t[:, b:b + 1], (queries, LANES))

    tile = 64
    halves = 2
    def weights_step(step, carry):
        at = step // (queries // tile) * (halves * LANES)
        q0 = lax.rem(step, queries // tile) * tile
        at = pl.multiple_of(at, halves * LANES)
        q0 = pl.multiple_of(q0, tile)
        accs = [jnp.zeros((tile, LANES), jnp.float32) for _ in range(halves)]
        for b in range(trees):
            leaf = qb[b, pl.ds(q0, tile), :]
            weight = wb[b, pl.ds(q0, tile), :]
            for h in range(halves):
                row = rl_ref[b:b + 1, pl.ds(pl.multiple_of(at + h * LANES, LANES), LANES)]
                accs[h] = accs[h] + jnp.where(leaf == row, weight, 0.0)
        w_s[pl.ds(q0, tile), pl.ds(at, halves * LANES)] = jnp.concatenate(accs, axis=1).astype(jnp.bfloat16)
        return carry

    lax.fori_loop(0, (rows // (halves * LANES)) * (queries // tile), weights_step, 0)

    per_chunk = width // CHUNKS // GROUP

    def compute(c):
        def body(g, carry):
            for jj in range(GROUP):
                j = (c * per_chunk + g) * GROUP + jj
                xb = jnp.broadcast_to(xf[pl.ds(j, 1), :], (16, rows)).astype(jnp.bfloat16)
                for k in range(0, width, 16):
                    prod[jj * width + k:jj * width + k + 16, :] = x_ref[k:k + 16, :] * xb
            res = lax.dot_general(w_s[...], prod[...], (((1,), (1,)), ((), ())),
                                  preferred_element_type=jnp.float32)
            off = pl.multiple_of(g * GROUP * width, GROUP * width)
            for a in range(2):
                for b in range(2):
                    part[c, a, b, :, pl.ds(off, GROUP * width)] = res[(a * 2 + b) * sub:(a * 2 + b + 1) * sub, :]
            return carry
        lax.fori_loop(0, per_chunk, body, 0)

    def copy(src, dst, ssem, rsem, peer):
        return pltpu.make_async_remote_copy(src_ref=src, dst_ref=dst, send_sem=ssem, recv_sem=rsem,
                                            device_id={"rows": peer}, device_id_type=pl.DeviceIdType.MESH)

    def c1(c):
        return copy(part.at[c, 1 - core], r1.at[c], ss1.at[c], rs1.at[c], sibling)

    def c2(c):
        return copy(s2.at[c], r2.at[c], ss2.at[c], rs2.at[c], ypeer)

    def c3(c, d):
        return copy(s3.at[c, lax.rem(z + d, nz)], r3.at[c, d - 1], ss3.at[c, d - 1], rs3.at[c, d - 1], zpeers[d - 1])

    def stage2(c):
        c1(c).wait_recv()
        s2[c] = part[c, core, 1 - y] + r1[c, 1 - y]
        c2(c).start()

    def stage3(c):
        c2(c).wait_recv()
        total = part[c, core, y] + r1[c, y] + r2[c]
        for k in range(nz):
            s3[c, k] = total[k * t:(k + 1) * t, :]
        for d in range(1, nz):
            c3(c, d).start()

    def finish(c):
        total = s3[c, z]
        for d in range(1, nz):
            c3(c, d).wait_recv()
            total = total + r3[c, d - 1]
        o_ref[:, c * cols:(c + 1) * cols] = total

    for s in range(CHUNKS + 3):
        if s < CHUNKS:
            compute(s)
            if s == 0:
                pl.semaphore_wait(barrier, 1 + nz)
            c1(s).start()
        if 0 <= s - 1 < CHUNKS:
            stage2(s - 1)
        if 0 <= s - 2 < CHUNKS:
            stage3(s - 2)
        if 0 <= s - 3 < CHUNKS:
            finish(s - 3)
    for c in range(CHUNKS):
        c1(c).wait_send()
        c2(c).wait_send()
        for d in range(1, nz):
            c3(c, d).wait_send()


def per_device(row_leaves, covariates, query_leaves, leaf_sizes):
    n = lax.axis_size("rows")
    trees, rows = row_leaves.shape
    width = covariates.shape[0]
    queries = query_leaves.shape[1]
    t = queries // n
    nz = n // 4
    sub = nz * t
    cols = width * width // CHUNKS
    vmem = pl.BlockSpec(memory_space=pltpu.VMEM)
    f32 = jnp.float32
    dma = pltpu.SemaphoreType.DMA
    return pl.pallas_call(
        functools.partial(kernel, n),
        out_shape=jax.ShapeDtypeStruct((t, width * width), f32),
        in_specs=[vmem] * 4,
        out_specs=vmem,
        scratch_shapes=[
            pltpu.VMEM((width, rows), f32),
            pltpu.VMEM((trees, queries, LANES), jnp.int32),
            pltpu.VMEM((trees, queries, LANES), f32),
            pltpu.VMEM((queries, rows), jnp.bfloat16),
            pltpu.VMEM((GROUP * width, rows), jnp.bfloat16),
            pltpu.VMEM((CHUNKS, 2, 2, sub, cols), f32),
            pltpu.VMEM((CHUNKS, sub, cols), f32),
            pltpu.VMEM((CHUNKS, nz, t, cols), f32),
            pltpu.VMEM((CHUNKS, 2, sub, cols), f32),
            pltpu.VMEM((CHUNKS, sub, cols), f32),
            pltpu.VMEM((CHUNKS, nz - 1, t, cols), f32),
            dma((CHUNKS,)), dma((CHUNKS,)), dma((CHUNKS,)), dma((CHUNKS,)),
            dma((CHUNKS, nz - 1)), dma((CHUNKS, nz - 1)),
        ],
        compiler_params=pltpu.CompilerParams(collective_id=0, has_side_effects=True,
                                             vmem_limit_bytes=56 << 20),
    )(row_leaves, covariates, query_leaves, leaf_sizes)


def solution(mesh):
    return jax.shard_map(
        per_device,
        mesh=mesh,
        in_specs=(
            P(None, ("groups", "rows")),
            P(None, ("groups", "rows")),
            P(None, "groups"),
            P("groups", None),
        ),
        out_specs=P(("groups", "rows"), None),
        check_vma=False,
    )
```

```python
import functools

import jax
import jax.numpy as jnp
from jax import lax
from jax.experimental import pallas as pl
from jax.experimental.pallas import tpu as pltpu
from jax.sharding import PartitionSpec as P

CHUNKS = 4
GROUP = 4
EARLY = 2
LANES = 128


def coded(value):
    largest = jnp.maximum(jnp.max(jnp.abs(value), axis=1, keepdims=True), 1e-30)
    power = jnp.floor(256.0 * jnp.log2(32000.0 / largest))
    whole = jnp.round(value * jnp.exp2(power * (1.0 / 256.0))).astype(jnp.int32)
    tail = jnp.broadcast_to(power.astype(jnp.int32), (value.shape[0], LANES))
    return jnp.concatenate([whole, tail], axis=1)


def decoded(code):
    wide = code.astype(jnp.int32).astype(jnp.float32)
    cols = wide.shape[1] - LANES
    return wide[:, :cols] * jnp.exp2(wide[:, cols:cols + 1] * (-1.0 / 256.0))


def kernel(n, rl_ref, x_ref, ql_ref, ls_ref, o_ref, xf, qb, wb, w_s, prod, part, own, s3, r1, r3,
           ss1, rs1, ss3, rs3):
    trees, rows = rl_ref.shape
    width = x_ref.shape[0]
    queries = ql_ref.shape[1]
    t = queries // n
    nz = n // 2
    sub = nz * t
    cols = width * width // CHUNKS
    me = lax.axis_index("rows")
    core = lax.rem(me, 2)
    z = me // 2
    sibling = me + 1 - 2 * core
    zpeers = [lax.rem(me + 2 * d, n) for d in range(1, nz)]
    barrier = pltpu.get_barrier_semaphore()
    for peer in [sibling] + zpeers:
        pl.semaphore_signal(barrier, inc=1, device_id={"rows": peer}, device_id_type=pl.DeviceIdType.MESH)

    xf[...] = x_ref[...].astype(jnp.float32)

    inverse = 1.0 / (trees * ls_ref[...].astype(jnp.float32))
    ql = ql_ref[...]
    leaf_cols, weight_cols = [], []
    for first in range(0, queries, LANES):
        piece = ql[:, first:first + LANES]
        if piece.shape[1] < LANES:
            piece = jnp.concatenate([piece] * (LANES // piece.shape[1]), axis=1)
        chosen = jnp.take_along_axis(inverse, piece, axis=1).astype(jnp.bfloat16).astype(jnp.float32)
        leaf_cols.append(piece.T)
        weight_cols.append(chosen.T)

    def ordered(cols_list):
        out = []
        for c in range(2):
            for k in range(nz):
                first = (k * 2 + c) * t
                out.append(cols_list[first // LANES][first % LANES:first % LANES + t])
        return jnp.concatenate(out, axis=0)

    leaf_t = ordered(leaf_cols)
    weight_t = ordered(weight_cols)
    for b in range(trees):
        qb[b] = jnp.broadcast_to(leaf_t[:, b:b + 1], (queries, LANES))
        wb[b] = jnp.broadcast_to(weight_t[:, b:b + 1], (queries, LANES))

    tile = 64
    halves = 2
    def weights_step(step, carry):
        at = step // (queries // tile) * (halves * LANES)
        q0 = lax.rem(step, queries // tile) * tile
        at = pl.multiple_of(at, halves * LANES)
        q0 = pl.multiple_of(q0, tile)
        accs = [jnp.zeros((tile, LANES), jnp.float32) for _ in range(halves)]
        for b in range(trees):
            leaf = qb[b, pl.ds(q0, tile), :]
            weight = wb[b, pl.ds(q0, tile), :]
            for h in range(halves):
                row = rl_ref[b:b + 1, pl.ds(pl.multiple_of(at + h * LANES, LANES), LANES)]
                accs[h] = accs[h] + jnp.where(leaf == row, weight, 0.0)
        w_s[pl.ds(q0, tile), pl.ds(at, halves * LANES)] = jnp.concatenate(accs, axis=1).astype(jnp.bfloat16)
        return carry

    lax.fori_loop(0, (rows // (halves * LANES)) * (queries // tile), weights_step, 0)

    per_chunk = width // CHUNKS // GROUP

    def compute(c):
        def body(g, carry):
            for jj in range(GROUP):
                j = (c * per_chunk + g) * GROUP + jj
                xb = jnp.broadcast_to(xf[pl.ds(j, 1), :], (16, rows)).astype(jnp.bfloat16)
                for k in range(0, width, 16):
                    prod[jj * width + k:jj * width + k + 16, :] = x_ref[k:k + 16, :] * xb
            res = lax.dot_general(w_s[...], prod[...], (((1,), (1,)), ((), ())),
                                  preferred_element_type=jnp.float32)
            off = pl.multiple_of(g * GROUP * width, GROUP * width)
            for a in range(2):
                part[c, a, :, pl.ds(off, GROUP * width)] = res[a * sub:(a + 1) * sub, :]
            return carry
        lax.fori_loop(0, per_chunk, body, 0)

    def copy(src, dst, ssem, rsem, peer):
        return pltpu.make_async_remote_copy(src_ref=src, dst_ref=dst, send_sem=ssem, recv_sem=rsem,
                                            device_id={"rows": peer}, device_id_type=pl.DeviceIdType.MESH)

    def c1(c):
        return copy(part.at[c, 1 - core], r1.at[c], ss1.at[c], rs1.at[c], sibling)

    def c3(c, d):
        return copy(s3.at[c, lax.rem(z + d, nz)], r3.at[c, d - 1], ss3.at[c, d - 1], rs3.at[c, d - 1], zpeers[d - 1])

    def exchange(c):
        c1(c).wait_recv()
        total = part[c, core] + r1[c]
        code = coded(total)
        for k in range(nz):
            own[c, k] = total[k * t:(k + 1) * t, :]
            s3[c, k] = code[k * t:(k + 1) * t, :].astype(jnp.int16)
        for d in range(1, nz):
            c3(c, d).start()

    def finish(c):
        total = own[c, z]
        for d in range(1, nz):
            c3(c, d).wait_recv()
            total = total + decoded(r3[c, d - 1])
        o_ref[:, c * cols:(c + 1) * cols] = total

    for c in range(CHUNKS):
        compute(c)
        if c == EARLY - 1:
            pl.semaphore_wait(barrier, nz)
            for e in range(EARLY):
                c1(e).start()
        if c >= EARLY:
            c1(c).start()
            for e in (range(EARLY) if c == EARLY else [c - 1]):
                exchange(e)
    exchange(CHUNKS - 1)
    for c in range(CHUNKS):
        finish(c)
    for c in range(CHUNKS):
        c1(c).wait_send()
        for d in range(1, nz):
            c3(c, d).wait_send()


def per_device(row_leaves, covariates, query_leaves, leaf_sizes):
    n = lax.axis_size("rows")
    trees, rows = row_leaves.shape
    width = covariates.shape[0]
    queries = query_leaves.shape[1]
    t = queries // n
    nz = n // 2
    sub = nz * t
    cols = width * width // CHUNKS
    vmem = pl.BlockSpec(memory_space=pltpu.VMEM)
    f32 = jnp.float32
    dma = pltpu.SemaphoreType.DMA
    return pl.pallas_call(
        functools.partial(kernel, n),
        out_shape=jax.ShapeDtypeStruct((t, width * width), f32),
        in_specs=[vmem] * 4,
        out_specs=vmem,
        scratch_shapes=[
            pltpu.VMEM((width, rows), f32),
            pltpu.VMEM((trees, queries, LANES), jnp.int32),
            pltpu.VMEM((trees, queries, LANES), f32),
            pltpu.VMEM((queries, rows), jnp.bfloat16),
            pltpu.VMEM((GROUP * width, rows), jnp.bfloat16),
            pltpu.VMEM((CHUNKS, 2, sub, cols), f32),
            pltpu.VMEM((CHUNKS, nz, t, cols), f32),
            pltpu.VMEM((CHUNKS, nz, t, cols + LANES), jnp.int16),
            pltpu.VMEM((CHUNKS, sub, cols), f32),
            pltpu.VMEM((CHUNKS, nz - 1, t, cols + LANES), jnp.int16),
            dma((CHUNKS,)), dma((CHUNKS,)),
            dma((CHUNKS, nz - 1)), dma((CHUNKS, nz - 1)),
        ],
        compiler_params=pltpu.CompilerParams(collective_id=0, has_side_effects=True,
                                             vmem_limit_bytes=56 << 20),
    )(row_leaves, covariates, query_leaves, leaf_sizes)


def solution(mesh):
    return jax.shard_map(
        per_device,
        mesh=mesh,
        in_specs=(
            P(None, ("groups", "rows")),
            P(None, ("groups", "rows")),
            P(None, "groups"),
            P("groups", None),
        ),
        out_specs=P(("groups", "rows"), None),
        check_vma=False,
    )
```

```python
import functools

import jax
import jax.numpy as jnp
from jax import lax
from jax.experimental import pallas as pl
from jax.experimental.pallas import tpu as pltpu
from jax.sharding import PartitionSpec as P

CHUNKS = 2
SIDE = 16
EARLY = 1
LANES = 128


def blocks_of(width):
    count = width // SIDE
    return [(a, b) for a in range(count) for b in range(a, count)]


def coded(value):
    largest = jnp.maximum(jnp.max(jnp.abs(value), axis=1, keepdims=True), 1e-30)
    power = jnp.floor(256.0 * jnp.log2(32000.0 / largest))
    whole = jnp.round(value * jnp.exp2(power * (1.0 / 256.0))).astype(jnp.int32)
    tail = jnp.broadcast_to(power.astype(jnp.int32), (value.shape[0], LANES))
    return jnp.concatenate([whole, tail], axis=1)


def decoded(code):
    wide = code.astype(jnp.int32).astype(jnp.float32)
    cols = wide.shape[1] - LANES
    return wide[:, :cols] * jnp.exp2(wide[:, cols:cols + 1] * (-1.0 / 256.0))


def kernel(n, rl_ref, x_ref, ql_ref, ls_ref, o_ref, xf, qb, wb, w_s, prod, part, own, s3, r1, r3, grid, turn,
           ss1, rs1, ss3, rs3):
    trees, rows = rl_ref.shape
    width = x_ref.shape[0]
    queries = ql_ref.shape[1]
    t = queries // n
    nz = n // 2
    sub = nz * t
    per_chunk = len(blocks_of(width)) // CHUNKS
    cols = per_chunk * SIDE * SIDE
    me = lax.axis_index("rows")
    core = lax.rem(me, 2)
    z = me // 2
    sibling = me + 1 - 2 * core
    zpeers = [lax.rem(me + 2 * d, n) for d in range(1, nz)]
    barrier = pltpu.get_barrier_semaphore()
    for peer in [sibling] + zpeers:
        pl.semaphore_signal(barrier, inc=1, device_id={"rows": peer}, device_id_type=pl.DeviceIdType.MESH)

    xf[...] = x_ref[...].astype(jnp.float32)

    inverse = 1.0 / (trees * ls_ref[...].astype(jnp.float32))
    ql = ql_ref[...]
    leaf_cols, weight_cols = [], []
    for first in range(0, queries, LANES):
        piece = ql[:, first:first + LANES]
        if piece.shape[1] < LANES:
            piece = jnp.concatenate([piece] * (LANES // piece.shape[1]), axis=1)
        chosen = jnp.take_along_axis(inverse, piece, axis=1).astype(jnp.bfloat16).astype(jnp.float32)
        leaf_cols.append(piece.T)
        weight_cols.append(chosen.T)

    def ordered(cols_list):
        out = []
        for c in range(2):
            for k in range(nz):
                first = (k * 2 + c) * t
                out.append(cols_list[first // LANES][first % LANES:first % LANES + t])
        return jnp.concatenate(out, axis=0)

    leaf_t = ordered(leaf_cols)
    weight_t = ordered(weight_cols)
    for b in range(trees):
        qb[b] = jnp.broadcast_to(leaf_t[:, b:b + 1], (queries, LANES))
        wb[b] = jnp.broadcast_to(weight_t[:, b:b + 1], (queries, LANES))

    tile = 64
    halves = 2
    def weights_step(step, carry):
        at = step // (queries // tile) * (halves * LANES)
        q0 = lax.rem(step, queries // tile) * tile
        at = pl.multiple_of(at, halves * LANES)
        q0 = pl.multiple_of(q0, tile)
        accs = [jnp.zeros((tile, LANES), jnp.float32) for _ in range(halves)]
        for b in range(trees):
            leaf = qb[b, pl.ds(q0, tile), :]
            weight = wb[b, pl.ds(q0, tile), :]
            for h in range(halves):
                row = rl_ref[b:b + 1, pl.ds(pl.multiple_of(at + h * LANES, LANES), LANES)]
                accs[h] = accs[h] + jnp.where(leaf == row, weight, 0.0)
        w_s[pl.ds(q0, tile), pl.ds(at, halves * LANES)] = jnp.concatenate(accs, axis=1).astype(jnp.bfloat16)
        return carry

    lax.fori_loop(0, (rows // (halves * LANES)) * (queries // tile), weights_step, 0)

    blocks = blocks_of(width)
    area = SIDE * SIDE

    def compute(c):
        for g in range(per_chunk):
            first, second = blocks[c * per_chunk + g]
            right = x_ref[second * SIDE:(second + 1) * SIDE, :]
            for jj in range(SIDE):
                j = first * SIDE + jj
                xb = jnp.broadcast_to(xf[j:j + 1, :], (SIDE, rows)).astype(jnp.bfloat16)
                prod[g % 2, jj * SIDE:(jj + 1) * SIDE, :] = right * xb
            res = lax.dot_general(w_s[...], prod[g % 2], (((1,), (1,)), ((), ())),
                                  preferred_element_type=jnp.float32)
            for a in range(2):
                part[c, a, :, g * area:(g + 1) * area] = res[a * sub:(a + 1) * sub, :]

    def copy(src, dst, ssem, rsem, peer):
        return pltpu.make_async_remote_copy(src_ref=src, dst_ref=dst, send_sem=ssem, recv_sem=rsem,
                                            device_id={"rows": peer}, device_id_type=pl.DeviceIdType.MESH)

    def c1(c):
        return copy(part.at[c, 1 - core], r1.at[c], ss1.at[c], rs1.at[c], sibling)

    def c3(c, d):
        return copy(s3.at[c, lax.rem(z + d, nz)], r3.at[c, d - 1], ss3.at[c, d - 1], rs3.at[c, d - 1], zpeers[d - 1])

    def exchange(c):
        c1(c).wait_recv()
        total = part[c, core] + r1[c]
        code = coded(total)
        for k in range(nz):
            own[c, k] = total[k * t:(k + 1) * t, :]
            s3[c, k] = code[k * t:(k + 1) * t, :].astype(jnp.int16)
        for d in range(1, nz):
            c3(c, d).start()

    count = width // SIDE

    def finish(c):
        total = own[c, z]
        for d in range(1, nz):
            c3(c, d).wait_recv()
            total = total + decoded(r3[c, d - 1])
        for g in range(per_chunk):
            a, b = blocks[c * per_chunk + g]
            block = total[:, g * area:(g + 1) * area]
            grid[b, a * t:(a + 1) * t, :] = block
            if a != b:
                at = upper.index((a, b)) * t
                turn[at:at + t, :] = block

    upper = [(a, b) for a, b in blocks if a != b]

    def mirror():
        value = turn[...]
        source = lax.broadcasted_iota(jnp.int32, (area, area), 0)
        target = lax.broadcasted_iota(jnp.int32, (area, area), 1)
        swap = jnp.where(source == lax.rem(target, SIDE) * SIDE + target // SIDE, 1.0, 0.0).astype(jnp.bfloat16)
        turned = jnp.zeros(value.shape, jnp.float32)
        for _ in range(3):
            piece = value.astype(jnp.bfloat16)
            turned = turned + jnp.dot(piece, swap, preferred_element_type=jnp.float32)
            value = value - piece.astype(jnp.float32)
        for i, (a, b) in enumerate(upper):
            grid[a, b * t:(b + 1) * t, :] = turned[i * t:(i + 1) * t, :]
        lane = lax.broadcasted_iota(jnp.int32, (count * t, LANES), 1)
        group = lax.rem(lane, width) // SIDE
        for tile_at in range(SIDE * width // LANES):
            per_tile = LANES // width
            src = tile_at * per_tile * SIDE
            pick = src % LANES + lane // width * SIDE + lax.rem(lane, SIDE)
            base = src // LANES * LANES
            out = jnp.zeros((count * t, LANES), jnp.float32)
            for b in range(count):
                out = jnp.where(group == b, jnp.take_along_axis(grid[b, :, base:base + LANES], pick, axis=1), out)
            for a in range(count):
                at = a * SIDE * width + tile_at * LANES
                o_ref[:, at:at + LANES] = out[a * t:(a + 1) * t, :]

    for c in range(CHUNKS):
        compute(c)
        if c == EARLY - 1:
            pl.semaphore_wait(barrier, nz)
            for e in range(EARLY):
                c1(e).start()
        if c >= EARLY:
            c1(c).start()
            for e in (range(EARLY) if c == EARLY else [c - 1]):
                exchange(e)
    exchange(CHUNKS - 1)
    for c in range(CHUNKS):
        finish(c)
    mirror()
    for c in range(CHUNKS):
        c1(c).wait_send()
        for d in range(1, nz):
            c3(c, d).wait_send()


def per_device(row_leaves, covariates, query_leaves, leaf_sizes):
    n = lax.axis_size("rows")
    trees, rows = row_leaves.shape
    width = covariates.shape[0]
    queries = query_leaves.shape[1]
    t = queries // n
    nz = n // 2
    sub = nz * t
    per_chunk = len(blocks_of(width)) // CHUNKS
    cols = per_chunk * SIDE * SIDE
    count = width // SIDE
    vmem = pl.BlockSpec(memory_space=pltpu.VMEM)
    f32 = jnp.float32
    dma = pltpu.SemaphoreType.DMA
    return pl.pallas_call(
        functools.partial(kernel, n),
        out_shape=jax.ShapeDtypeStruct((t, width * width), f32),
        in_specs=[vmem] * 4,
        out_specs=vmem,
        scratch_shapes=[
            pltpu.VMEM((width, rows), f32),
            pltpu.VMEM((trees, queries, LANES), jnp.int32),
            pltpu.VMEM((trees, queries, LANES), f32),
            pltpu.VMEM((queries, rows), jnp.bfloat16),
            pltpu.VMEM((2, SIDE * SIDE, rows), jnp.bfloat16),
            pltpu.VMEM((CHUNKS, 2, sub, cols), f32),
            pltpu.VMEM((CHUNKS, nz, t, cols), f32),
            pltpu.VMEM((CHUNKS, nz, t, cols + LANES), jnp.int16),
            pltpu.VMEM((CHUNKS, sub, cols), f32),
            pltpu.VMEM((CHUNKS, nz - 1, t, cols + LANES), jnp.int16),
            pltpu.VMEM((count, count * t, SIDE * SIDE), f32),
            pltpu.VMEM((count * (count - 1) // 2 * t, SIDE * SIDE), f32),
            dma((CHUNKS,)), dma((CHUNKS,)),
            dma((CHUNKS, nz - 1)), dma((CHUNKS, nz - 1)),
        ],
        compiler_params=pltpu.CompilerParams(collective_id=0, has_side_effects=True,
                                             vmem_limit_bytes=56 << 20),
    )(row_leaves, covariates, query_leaves, leaf_sizes)


def solution(mesh):
    return jax.shard_map(
        per_device,
        mesh=mesh,
        in_specs=(
            P(None, ("groups", "rows")),
            P(None, ("groups", "rows")),
            P(None, "groups"),
            P("groups", None),
        ),
        out_specs=P(("groups", "rows"), None),
        check_vma=False,
    )
```

```python
import functools

import jax
import jax.numpy as jnp
from jax import lax
from jax.experimental import pallas as pl
from jax.experimental.pallas import tpu as pltpu
from jax.sharding import PartitionSpec as P

CHUNKS = 1
SIDE = 16
LANES = 128


def blocks_of(width):
    count = width // SIDE
    return [(a, b) for a in range(count) for b in range(a, count)]


def coded(value):
    largest = jnp.maximum(jnp.max(jnp.abs(value), axis=1, keepdims=True), 1e-30)
    power = jnp.floor(256.0 * jnp.log2(32000.0 / largest))
    whole = jnp.round(value * jnp.exp2(power * (1.0 / 256.0))).astype(jnp.int32)
    tail = jnp.broadcast_to(power.astype(jnp.int32), (value.shape[0], LANES))
    return jnp.concatenate([whole, tail], axis=1)


def decoded(code):
    wide = code.astype(jnp.int32).astype(jnp.float32)
    cols = wide.shape[1] - LANES
    return wide[:, :cols] * jnp.exp2(wide[:, cols:cols + 1] * (-1.0 / 256.0))


def kernel(n, rl_ref, x_ref, ql_ref, ls_ref, o_ref, xf, qb, wb, w_s, prod, part, own, s3, r1, r3, grid, turn,
           ss1, rs1, ss3, rs3):
    trees, rows = rl_ref.shape
    width = x_ref.shape[0]
    queries = ql_ref.shape[1]
    t = queries // n
    nz = n // 2
    sub = nz * t
    per_chunk = len(blocks_of(width)) // CHUNKS
    cols = per_chunk * SIDE * SIDE
    me = lax.axis_index("rows")
    core = lax.rem(me, 2)
    z = me // 2
    sibling = me + 1 - 2 * core
    zpeers = [lax.rem(me + 2 * d, n) for d in range(1, nz)]
    barrier = pltpu.get_barrier_semaphore()
    for peer in [sibling] + zpeers:
        pl.semaphore_signal(barrier, inc=1, device_id={"rows": peer}, device_id_type=pl.DeviceIdType.MESH)

    xf[...] = x_ref[...].astype(jnp.float32)

    inverse = 1.0 / (trees * ls_ref[...].astype(jnp.float32))
    ql = ql_ref[...]
    leaf_cols, weight_cols = [], []
    for first in range(0, queries, LANES):
        piece = ql[:, first:first + LANES]
        if piece.shape[1] < LANES:
            piece = jnp.concatenate([piece] * (LANES // piece.shape[1]), axis=1)
        chosen = jnp.take_along_axis(inverse, piece, axis=1).astype(jnp.bfloat16).astype(jnp.float32)
        leaf_cols.append(piece.T)
        weight_cols.append(chosen.T)

    def ordered(cols_list):
        out = []
        for c in range(2):
            for k in range(nz):
                first = (k * 2 + c) * t
                out.append(cols_list[first // LANES][first % LANES:first % LANES + t])
        return jnp.concatenate(out, axis=0)

    leaf_t = ordered(leaf_cols)
    weight_t = ordered(weight_cols)
    for b in range(trees):
        qb[b] = jnp.broadcast_to(leaf_t[:, b:b + 1], (queries, LANES))
        wb[b] = jnp.broadcast_to(weight_t[:, b:b + 1], (queries, LANES))

    tile = 64
    halves = 2
    def weights_step(step, carry):
        at = step // (queries // tile) * (halves * LANES)
        q0 = lax.rem(step, queries // tile) * tile
        at = pl.multiple_of(at, halves * LANES)
        q0 = pl.multiple_of(q0, tile)
        accs = [jnp.zeros((tile, LANES), jnp.float32) for _ in range(halves)]
        for b in range(trees):
            leaf = qb[b, pl.ds(q0, tile), :]
            weight = wb[b, pl.ds(q0, tile), :]
            for h in range(halves):
                row = rl_ref[b:b + 1, pl.ds(pl.multiple_of(at + h * LANES, LANES), LANES)]
                accs[h] = accs[h] + jnp.where(leaf == row, weight, 0.0)
        w_s[pl.ds(q0, tile), pl.ds(at, halves * LANES)] = jnp.concatenate(accs, axis=1).astype(jnp.bfloat16)
        return carry

    lax.fori_loop(0, (rows // (halves * LANES)) * (queries // tile), weights_step, 0)

    blocks = blocks_of(width)
    area = SIDE * SIDE

    def compute(c):
        for g in range(per_chunk):
            first, second = blocks[c * per_chunk + g]
            right = x_ref[second * SIDE:(second + 1) * SIDE, :]
            for jj in range(SIDE):
                j = first * SIDE + jj
                xb = jnp.broadcast_to(xf[j:j + 1, :], (SIDE, rows)).astype(jnp.bfloat16)
                prod[g % 2, jj * SIDE:(jj + 1) * SIDE, :] = right * xb
            res = lax.dot_general(w_s[...], prod[g % 2], (((1,), (1,)), ((), ())),
                                  preferred_element_type=jnp.float32)
            for a in range(2):
                part[c, a, :, g * area:(g + 1) * area] = res[a * sub:(a + 1) * sub, :]

    def copy(src, dst, ssem, rsem, peer):
        return pltpu.make_async_remote_copy(src_ref=src, dst_ref=dst, send_sem=ssem, recv_sem=rsem,
                                            device_id={"rows": peer}, device_id_type=pl.DeviceIdType.MESH)

    def c1(c):
        return copy(part.at[c, 1 - core], r1.at[c], ss1.at[c], rs1.at[c], sibling)

    def c3(c, d):
        return copy(s3.at[c, lax.rem(z + d, nz)], r3.at[c, d - 1], ss3.at[c, d - 1], rs3.at[c, d - 1], zpeers[d - 1])

    def exchange(c):
        c1(c).wait_recv()
        total = part[c, core] + r1[c]
        code = coded(total)
        for k in range(nz):
            own[c, k] = total[k * t:(k + 1) * t, :]
            s3[c, k] = code[k * t:(k + 1) * t, :].astype(jnp.int16)
        for d in range(1, nz):
            c3(c, d).start()

    count = width // SIDE

    def finish(c):
        total = own[c, z]
        for d in range(1, nz):
            c3(c, d).wait_recv()
            total = total + decoded(r3[c, d - 1])
        for g in range(per_chunk):
            a, b = blocks[c * per_chunk + g]
            block = total[:, g * area:(g + 1) * area]
            grid[b, a * t:(a + 1) * t, :] = block
            if a != b:
                at = upper.index((a, b)) * t
                turn[at:at + t, :] = block

    upper = [(a, b) for a, b in blocks if a != b]

    def mirror():
        value = turn[...]
        source = lax.broadcasted_iota(jnp.int32, (area, area), 0)
        target = lax.broadcasted_iota(jnp.int32, (area, area), 1)
        swap = jnp.where(source == lax.rem(target, SIDE) * SIDE + target // SIDE, 1.0, 0.0).astype(jnp.bfloat16)
        turned = jnp.zeros(value.shape, jnp.float32)
        for _ in range(3):
            piece = value.astype(jnp.bfloat16)
            turned = turned + jnp.dot(piece, swap, preferred_element_type=jnp.float32)
            value = value - piece.astype(jnp.float32)
        for i, (a, b) in enumerate(upper):
            grid[a, b * t:(b + 1) * t, :] = turned[i * t:(i + 1) * t, :]
        lane = lax.broadcasted_iota(jnp.int32, (count * t, LANES), 1)
        group = lax.rem(lane, width) // SIDE
        for tile_at in range(SIDE * width // LANES):
            per_tile = LANES // width
            src = tile_at * per_tile * SIDE
            pick = src % LANES + lane // width * SIDE + lax.rem(lane, SIDE)
            base = src // LANES * LANES
            out = jnp.zeros((count * t, LANES), jnp.float32)
            for b in range(count):
                out = jnp.where(group == b, jnp.take_along_axis(grid[b, :, base:base + LANES], pick, axis=1), out)
            for a in range(count):
                at = a * SIDE * width + tile_at * LANES
                o_ref[:, at:at + LANES] = out[a * t:(a + 1) * t, :]

    for c in range(CHUNKS):
        compute(c)
    pl.semaphore_wait(barrier, nz)
    for c in range(CHUNKS):
        c1(c).start()
    for c in range(CHUNKS):
        exchange(c)
    for c in range(CHUNKS):
        finish(c)
    mirror()
    for c in range(CHUNKS):
        c1(c).wait_send()
        for d in range(1, nz):
            c3(c, d).wait_send()


def per_device(row_leaves, covariates, query_leaves, leaf_sizes):
    n = lax.axis_size("rows")
    trees, rows = row_leaves.shape
    width = covariates.shape[0]
    queries = query_leaves.shape[1]
    t = queries // n
    nz = n // 2
    sub = nz * t
    per_chunk = len(blocks_of(width)) // CHUNKS
    cols = per_chunk * SIDE * SIDE
    count = width // SIDE
    vmem = pl.BlockSpec(memory_space=pltpu.VMEM)
    f32 = jnp.float32
    dma = pltpu.SemaphoreType.DMA
    return pl.pallas_call(
        functools.partial(kernel, n),
        out_shape=jax.ShapeDtypeStruct((t, width * width), f32),
        in_specs=[vmem] * 4,
        out_specs=vmem,
        scratch_shapes=[
            pltpu.VMEM((width, rows), f32),
            pltpu.VMEM((trees, queries, LANES), jnp.int32),
            pltpu.VMEM((trees, queries, LANES), f32),
            pltpu.VMEM((queries, rows), jnp.bfloat16),
            pltpu.VMEM((2, SIDE * SIDE, rows), jnp.bfloat16),
            pltpu.VMEM((CHUNKS, 2, sub, cols), f32),
            pltpu.VMEM((CHUNKS, nz, t, cols), f32),
            pltpu.VMEM((CHUNKS, nz, t, cols + LANES), jnp.int16),
            pltpu.VMEM((CHUNKS, sub, cols), f32),
            pltpu.VMEM((CHUNKS, nz - 1, t, cols + LANES), jnp.int16),
            pltpu.VMEM((count, count * t, SIDE * SIDE), f32),
            pltpu.VMEM((count * (count - 1) // 2 * t, SIDE * SIDE), f32),
            dma((CHUNKS,)), dma((CHUNKS,)),
            dma((CHUNKS, nz - 1)), dma((CHUNKS, nz - 1)),
        ],
        compiler_params=pltpu.CompilerParams(collective_id=0, has_side_effects=True,
                                             vmem_limit_bytes=56 << 20),
    )(row_leaves, covariates, query_leaves, leaf_sizes)


def solution(mesh):
    return jax.shard_map(
        per_device,
        mesh=mesh,
        in_specs=(
            P(None, ("groups", "rows")),
            P(None, ("groups", "rows")),
            P(None, "groups"),
            P("groups", None),
        ),
        out_specs=P(("groups", "rows"), None),
        check_vma=False,
    )
```

```python
import functools

import jax
import jax.numpy as jnp
from jax import lax
from jax.experimental import pallas as pl
from jax.experimental.pallas import tpu as pltpu
from jax.sharding import PartitionSpec as P

CHUNKS = 1
SIDE = 16
LANES = 128


def blocks_of(width):
    count = width // SIDE
    return [(a, b) for a in range(count) for b in range(a, count)]


def coded(value):
    largest = jnp.maximum(jnp.max(jnp.abs(value), axis=1, keepdims=True), 1e-30)
    power = jnp.floor(256.0 * jnp.log2(32000.0 / largest))
    whole = jnp.round(value * jnp.exp2(power * (1.0 / 256.0))).astype(jnp.int32)
    tail = jnp.broadcast_to(power.astype(jnp.int32), (value.shape[0], LANES))
    return jnp.concatenate([whole, tail], axis=1)


def decoded(code):
    wide = code.astype(jnp.int32).astype(jnp.float32)
    cols = wide.shape[1] - LANES
    return wide[:, :cols] * jnp.exp2(wide[:, cols:cols + 1] * (-1.0 / 256.0))


def kernel(n, rl_ref, x_ref, ql_ref, ls_ref, o_ref, xf, qb, wb, w_s, prod, part, own, s3, r1, r3, grid, turn,
           ss1, rs1, ss3, rs3):
    trees, rows = rl_ref.shape
    width = x_ref.shape[0]
    queries = ql_ref.shape[1]
    t = queries // n
    nz = n // 2
    sub = nz * t
    per_chunk = len(blocks_of(width)) // CHUNKS
    cols = per_chunk * SIDE * SIDE
    me = lax.axis_index("rows")
    core = lax.rem(me, 2)
    z = me // 2
    sibling = me + 1 - 2 * core
    zpeers = [lax.rem(me + 2 * d, n) for d in range(1, nz)]
    barrier = pltpu.get_barrier_semaphore()
    for peer in [sibling] + zpeers:
        pl.semaphore_signal(barrier, inc=1, device_id={"rows": peer}, device_id_type=pl.DeviceIdType.MESH)

    xf[...] = x_ref[...].astype(jnp.float32)

    inverse = 1.0 / (trees * ls_ref[...].astype(jnp.float32))
    ql = ql_ref[...]
    leaf_cols, weight_cols = [], []
    for first in range(0, queries, LANES):
        piece = ql[:, first:first + LANES]
        if piece.shape[1] < LANES:
            piece = jnp.concatenate([piece] * (LANES // piece.shape[1]), axis=1)
        chosen = jnp.take_along_axis(inverse, piece, axis=1).astype(jnp.bfloat16).astype(jnp.float32)
        leaf_cols.append(piece.T)
        weight_cols.append(chosen.T)

    def ordered(cols_list):
        out = []
        for c in range(2):
            for k in range(nz):
                first = (k * 2 + c) * t
                out.append(cols_list[first // LANES][first % LANES:first % LANES + t])
        return jnp.concatenate(out, axis=0)

    leaf_t = ordered(leaf_cols)
    weight_t = ordered(weight_cols)
    for b in range(trees):
        qb[b] = jnp.broadcast_to(leaf_t[:, b:b + 1], (queries, LANES))
        wb[b] = jnp.broadcast_to(weight_t[:, b:b + 1], (queries, LANES))

    tile = 64
    halves = 2
    def weights_step(step, carry):
        at = step // (queries // tile) * (halves * LANES)
        q0 = lax.rem(step, queries // tile) * tile
        at = pl.multiple_of(at, halves * LANES)
        q0 = pl.multiple_of(q0, tile)
        accs = [jnp.zeros((tile, LANES), jnp.float32) for _ in range(halves)]
        for b in range(trees):
            leaf = qb[b, pl.ds(q0, tile), :]
            weight = wb[b, pl.ds(q0, tile), :]
            for h in range(halves):
                row = rl_ref[b:b + 1, pl.ds(pl.multiple_of(at + h * LANES, LANES), LANES)]
                accs[h] = accs[h] + jnp.where(leaf == row, weight, 0.0)
        w_s[pl.ds(q0, tile), pl.ds(at, halves * LANES)] = jnp.concatenate(accs, axis=1).astype(jnp.bfloat16)
        return carry

    lax.fori_loop(0, (rows // (halves * LANES)) * (queries // tile), weights_step, 0)

    blocks = blocks_of(width)
    area = SIDE * SIDE

    def compute(c):
        for g in range(per_chunk):
            first, second = blocks[c * per_chunk + g]
            right = x_ref[second * SIDE:(second + 1) * SIDE, :]
            for jj in range(SIDE):
                j = first * SIDE + jj
                xb = jnp.broadcast_to(xf[j:j + 1, :], (SIDE, rows)).astype(jnp.bfloat16)
                prod[g % 2, jj * SIDE:(jj + 1) * SIDE, :] = right * xb
            res = lax.dot_general(w_s[...], prod[g % 2], (((1,), (1,)), ((), ())),
                                  preferred_element_type=jnp.float32)
            for a in range(2):
                part[c, a, :, g * area:(g + 1) * area] = res[a * sub:(a + 1) * sub, :]

    def copy(src, dst, ssem, rsem, peer):
        return pltpu.make_async_remote_copy(src_ref=src, dst_ref=dst, send_sem=ssem, recv_sem=rsem,
                                            device_id={"rows": peer}, device_id_type=pl.DeviceIdType.MESH)

    def c1(c):
        return copy(part.at[c, 1 - core], r1.at[c], ss1.at[c], rs1.at[c], sibling)

    def c3(c, d):
        return copy(s3.at[c, lax.rem(z + d, nz)], r3.at[c, d - 1], ss3.at[c, d - 1], rs3.at[c, d - 1], zpeers[d - 1])

    def exchange(c):
        c1(c).wait_recv()
        total = part[c, core] + r1[c]
        code = coded(total)
        for k in range(nz):
            own[c, k] = total[k * t:(k + 1) * t, :]
            s3[c, k] = code[k * t:(k + 1) * t, :].astype(jnp.int16)
        for d in sorted(range(1, nz), key=lambda d: abs(d - nz // 2)):
            c3(c, d).start()

    count = width // SIDE

    def finish(c):
        total = own[c, z]
        for d in range(1, nz):
            c3(c, d).wait_recv()
            total = total + decoded(r3[c, d - 1])
        for g in range(per_chunk):
            a, b = blocks[c * per_chunk + g]
            block = total[:, g * area:(g + 1) * area]
            grid[b, a * t:(a + 1) * t, :] = block
            if a != b:
                at = upper.index((a, b)) * t
                turn[at:at + t, :] = block

    upper = [(a, b) for a, b in blocks if a != b]

    def mirror():
        value = turn[...]
        source = lax.broadcasted_iota(jnp.int32, (area, area), 0)
        target = lax.broadcasted_iota(jnp.int32, (area, area), 1)
        swap = jnp.where(source == lax.rem(target, SIDE) * SIDE + target // SIDE, 1.0, 0.0).astype(jnp.bfloat16)
        turned = jnp.zeros(value.shape, jnp.float32)
        for _ in range(3):
            piece = value.astype(jnp.bfloat16)
            turned = turned + jnp.dot(piece, swap, preferred_element_type=jnp.float32)
            value = value - piece.astype(jnp.float32)
        for i, (a, b) in enumerate(upper):
            grid[a, b * t:(b + 1) * t, :] = turned[i * t:(i + 1) * t, :]
        lane = lax.broadcasted_iota(jnp.int32, (count * t, LANES), 1)
        group = lax.rem(lane, width) // SIDE
        for tile_at in range(SIDE * width // LANES):
            per_tile = LANES // width
            src = tile_at * per_tile * SIDE
            pick = src % LANES + lane // width * SIDE + lax.rem(lane, SIDE)
            base = src // LANES * LANES
            out = jnp.zeros((count * t, LANES), jnp.float32)
            for b in range(count):
                out = jnp.where(group == b, jnp.take_along_axis(grid[b, :, base:base + LANES], pick, axis=1), out)
            for a in range(count):
                at = a * SIDE * width + tile_at * LANES
                o_ref[:, at:at + LANES] = out[a * t:(a + 1) * t, :]

    for c in range(CHUNKS):
        compute(c)
    pl.semaphore_wait(barrier, nz)
    for c in range(CHUNKS):
        c1(c).start()
    for c in range(CHUNKS):
        exchange(c)
    for c in range(CHUNKS):
        finish(c)
    mirror()
    for c in range(CHUNKS):
        c1(c).wait_send()
        for d in range(1, nz):
            c3(c, d).wait_send()


def per_device(row_leaves, covariates, query_leaves, leaf_sizes):
    n = lax.axis_size("rows")
    trees, rows = row_leaves.shape
    width = covariates.shape[0]
    queries = query_leaves.shape[1]
    t = queries // n
    nz = n // 2
    sub = nz * t
    per_chunk = len(blocks_of(width)) // CHUNKS
    cols = per_chunk * SIDE * SIDE
    count = width // SIDE
    vmem = pl.BlockSpec(memory_space=pltpu.VMEM)
    f32 = jnp.float32
    dma = pltpu.SemaphoreType.DMA
    return pl.pallas_call(
        functools.partial(kernel, n),
        out_shape=jax.ShapeDtypeStruct((t, width * width), f32),
        in_specs=[vmem] * 4,
        out_specs=vmem,
        scratch_shapes=[
            pltpu.VMEM((width, rows), f32),
            pltpu.VMEM((trees, queries, LANES), jnp.int32),
            pltpu.VMEM((trees, queries, LANES), f32),
            pltpu.VMEM((queries, rows), jnp.bfloat16),
            pltpu.VMEM((2, SIDE * SIDE, rows), jnp.bfloat16),
            pltpu.VMEM((CHUNKS, 2, sub, cols), f32),
            pltpu.VMEM((CHUNKS, nz, t, cols), f32),
            pltpu.VMEM((CHUNKS, nz, t, cols + LANES), jnp.int16),
            pltpu.VMEM((CHUNKS, sub, cols), f32),
            pltpu.VMEM((CHUNKS, nz - 1, t, cols + LANES), jnp.int16),
            pltpu.VMEM((count, count * t, SIDE * SIDE), f32),
            pltpu.VMEM((count * (count - 1) // 2 * t, SIDE * SIDE), f32),
            dma((CHUNKS,)), dma((CHUNKS,)),
            dma((CHUNKS, nz - 1)), dma((CHUNKS, nz - 1)),
        ],
        compiler_params=pltpu.CompilerParams(collective_id=0, has_side_effects=True,
                                             vmem_limit_bytes=56 << 20),
    )(row_leaves, covariates, query_leaves, leaf_sizes)


def solution(mesh):
    return jax.shard_map(
        per_device,
        mesh=mesh,
        in_specs=(
            P(None, ("groups", "rows")),
            P(None, ("groups", "rows")),
            P(None, "groups"),
            P("groups", None),
        ),
        out_specs=P(("groups", "rows"), None),
        check_vma=False,
    )
```
